256 devices in a mesh: rows: 64 (over z, x, core), cols: 4 (over y).
Axes of the slice: x: 4, y: 4, z: 8, core: 2. Of those that a mesh axis runs over, the one named last changes fastest.
Arguments:
- embeddings: bfloat16 [65536, 512], P('rows'), may hold values from -90 to 90
- neighbours: int32 [256, 12], P('rows'), may hold values from -1 to 255, as said below
- queries: float32 [65536, 512], P('rows', 'cols'), may hold values from -22 to 22
Outputs:
- diffused: float32 [65536, 512], P('rows', 'cols')
The draws below stay inside these ranges and needn't reach their ends.
Inputs may be any that keep to these rules, and one draw needn't show every extreme that they name: `neighbours`: row b lists in rising order the distinct blocks linked to block b, then -1 in the remaining slots. Every block is linked to itself, links are symmetric, and a linked block lies on the same index of rows as b or on an adjacent one, block c lying on index c // 4. Some block has 12 links.
All inputs are finite; a program needn't handle non-finite values.
Results may differ from the reference program's by a relative error of at most 0.00039.
Values may be sent and summed in bfloat16 or wider, within the bound.
No kernel may reach another device: no remote copies, remote signals or barrier semaphores. Data moves between devices by JAX's collectives and lax.ppermute only.
A program may use at most 128 MiB of HBM per device.

```python
import math
import jax
import jax.numpy as jnp
from jax import lax

BLK = 256
D = 512
BLK_DEV = 4
ITERS = 3
KMAX = 12
NB = 256
N = 65536
Q = 512


def draw_neighbours(key, part):
    blocks = jnp.arange(NB, dtype=jnp.int32)
    owners = blocks // BLK_DEV
    propensity = jax.random.randint(jax.random.fold_in(key, 11), (NB,), 3, 11)
    chance = jax.random.randint(jax.random.fold_in(key, 12), (NB, NB), 0, 100)
    upper = blocks[:, None] < blocks[None, :]
    symmetric = jnp.where(upper, chance, chance.T)
    linked = symmetric < propensity[:, None] * propensity[None, :]
    nearby = jnp.abs(owners[:, None] - owners[None, :]) <= 1
    rims = (blocks[:, None] % BLK_DEV == 0) & (blocks[None, :] == blocks[:, None] - 1)
    rims = rims | rims.T
    hub_owner = jax.random.randint(jax.random.fold_in(key, 13), (), 1, NB // BLK_DEV - 1)
    hub_block = hub_owner * BLK_DEV + jax.random.randint(jax.random.fold_in(key, 14), (), 0, BLK_DEV)
    hubbed = (blocks[:, None] == hub_block) | (blocks[None, :] == hub_block)
    selfish = blocks[:, None] == blocks[None, :]
    links = nearby & (linked | rims | hubbed | selfish)
    scores = jnp.where(links, blocks[None, :], NB + blocks[None, :])
    ordered = jnp.sort(scores, axis=1)[:, :KMAX]
    return jnp.where(ordered < NB, ordered, -1).astype(jnp.int32)


def draw_embeddings(key, part):
    centres = jnp.clip(jax.random.normal(jax.random.fold_in(key, 21), (16, D), jnp.float32), -4.0, 4.0)
    labels = jax.random.randint(jax.random.fold_in(key, 22), (N,), 0, 16)
    strength = jax.random.uniform(jax.random.fold_in(key, 23), (N, 1), jnp.float32, 0.6, 1.2)
    noise = jnp.clip(jax.random.normal(jax.random.fold_in(key, 24), (N, D), jnp.float32), -5.0, 5.0)
    values = 1.2 * strength * centres[labels] + noise
    return values.astype(jnp.bfloat16)


def draw_queries(key, part):
    position = jnp.arange(N, dtype=jnp.float32) / N
    rising = jnp.exp(math.log(3.0) * position)[:, None]
    values = jnp.clip(jax.random.normal(jax.random.fold_in(key, 31), (N, Q), jnp.float32), -5.0, 5.0)
    return (values * rising).astype(jnp.float32)


def setup_inputs(seed: int = 0) -> dict:
    arg_keys = jax.random.split(jax.random.key(seed), 4)
    return {
        "embeddings": draw_embeddings(jax.random.fold_in(arg_keys[3], 71), 0),
        "neighbours": draw_neighbours(jax.random.fold_in(arg_keys[3], 71), 0),
        "queries": draw_queries(jax.random.fold_in(arg_keys[3], 71), 0),
    }


diffusion = 0.9
epsilon = 1e-06
highest = lax.Precision.HIGHEST

def normalize(embeddings):
    values = embeddings.astype(jnp.float32)
    scaled = values * lax.rsqrt(lax.optimization_barrier(jnp.sum(values * values, axis=1, keepdims=True)) + epsilon)
    return scaled.astype(jnp.bfloat16)

def reference(embeddings, neighbours, queries):
    normed = normalize(embeddings)
    blocks = normed.reshape(NB, BLK, D)
    valid = neighbours >= 0
    safe_ids = jnp.where(valid, neighbours, 0).astype(jnp.int32)

    def affinity_block(element):
        own_rows, block_ids, live = element
        others = blocks[block_ids].astype(jnp.float32)
        similar = jnp.einsum('id,kjd->ikj', own_rows.astype(jnp.float32), others, precision=highest)
        cubed = jnp.maximum(similar, 0.0) ** 3
        return cubed * live.astype(jnp.float32)[None, :, None]
    affinity = lax.map(affinity_block, (blocks, safe_ids, valid))
    degree = lax.optimization_barrier(jnp.sum(affinity, axis=(2, 3)))
    inv_root = lax.rsqrt(degree)
    graph = affinity * inv_root[:, :, None, None] * inv_root[safe_ids][:, None, :, :]

    def operate(direction):
        pieces = direction.reshape(NB, BLK, Q)

        def one_block(element):
            weights_row, block_ids = element
            gathered = pieces[block_ids]
            return jnp.einsum('ikj,kjq->iq', weights_row, gathered, precision=highest)
        mixed = lax.map(one_block, (graph, safe_ids)).reshape(N, Q)
        return direction - diffusion * mixed
    diffused = jnp.zeros_like(queries)
    residual = queries
    direction = queries
    residual_sq = lax.optimization_barrier(jnp.sum(residual * residual, axis=0))
    for iteration in range(ITERS):
        image = operate(direction)
        curvature = lax.optimization_barrier(jnp.sum(direction * image, axis=0))
        step_size = residual_sq / curvature
        diffused = diffused + step_size * direction
        residual = residual - step_size * image
        if iteration + 1 < ITERS:
            updated = lax.optimization_barrier(jnp.sum(residual * residual, axis=0))
            direction = residual + updated / residual_sq * direction
            residual_sq = updated
    return diffused
```

```python
import math

import jax
import jax.numpy as jnp
from jax import lax
from jax.experimental import pallas as pl
from jax.experimental.pallas import tpu as pltpu
from jax.sharding import Mesh, PartitionSpec as P

diffusion = 0.9
epsilon = 1e-06
tiny = 2e-07
f32 = jnp.float32
bf16 = jnp.bfloat16
ROWS = ("z", "x", "core")


def unit_rows(raw):
    values = raw.astype(f32)
    total = jnp.sum(values * values, axis=1, keepdims=True)
    return (values * lax.rsqrt(total + epsilon)).astype(bf16)


def affinity_kernel(linked, own_ref, other_ref, w_ref, deg_ref, unit_ref):
    step = pl.program_id(0)
    blocks = linked.shape[0]
    rows = own_ref.shape[0] // blocks

    @pl.when(step == 0)
    def _():
        unit_ref[...] = unit_rows(own_ref[...])
        deg_ref[...] = jnp.zeros_like(deg_ref)

    other = unit_rows(other_ref[...])
    for b in range(blocks):
        part = pl.ds(b * rows, rows)
        similar = lax.dot_general(
            unit_ref[part, :], other, (((1,), (1,)), ((), ())), preferred_element_type=f32
        )
        kept = jnp.maximum(similar, 0.0)
        w = kept * kept * (kept * linked[b, step])
        high = w.astype(bf16)
        w_ref[pl.ds(2 * b * rows, rows), :] = high
        w_ref[pl.ds((2 * b + 1) * rows, rows), :] = (w - high.astype(f32)).astype(bf16)
        half = w.shape[1] // 2
        deg_ref[part, :] += w[:, :half] + w[:, half:]


def affinity(own, other, linked):
    n, features = own.shape
    blocks = linked.shape[0]
    rows = n // blocks
    return pl.pallas_call(
        affinity_kernel,
        grid_spec=pltpu.PrefetchScalarGridSpec(
            num_scalar_prefetch=1,
            grid=(blocks,),
            in_specs=[
                pl.BlockSpec((n, features), lambda c, m: (0, 0)),
                pl.BlockSpec((rows, features), lambda c, m: (c, 0)),
            ],
            out_specs=[
                pl.BlockSpec((2 * n, rows), lambda c, m: (0, c)),
                pl.BlockSpec((n, 128), lambda c, m: (0, 0)),
            ],
            scratch_shapes=[pltpu.VMEM((n, features), bf16)],
        ),
        out_shape=[
            jax.ShapeDtypeStruct((2 * n, n), bf16),
            jax.ShapeDtypeStruct((n, 128), f32),
        ],
        cost_estimate=pl.CostEstimate(flops=2 * n * n * features, bytes_accessed=8 * n * n, transcendentals=0),
        compiler_params=pltpu.CompilerParams(vmem_limit_bytes=32 << 20),
    )(linked, own, other)


def product_kernel(w_ref, u_ref, base_ref, out_ref):
    rows, columns = out_ref.shape
    wide = jnp.dot(w_ref[...], u_ref[...], preferred_element_type=f32)
    both = wide[:rows] + wide[rows:]
    out_ref[...] = base_ref[...] + (both[:, :columns] + both[:, columns:])


def product(w, split, base):
    n, columns = base.shape
    rows = n // 4
    return pl.pallas_call(
        product_kernel,
        grid=(4,),
        in_specs=[
            pl.BlockSpec((2 * rows, n), lambda b: (b, 0)),
            pl.BlockSpec((n, 2 * columns), lambda b: (0, 0)),
            pl.BlockSpec((rows, columns), lambda b: (b, 0)),
        ],
        out_specs=pl.BlockSpec((rows, columns), lambda b: (b, 0)),
        out_shape=jax.ShapeDtypeStruct((n, columns), f32),
        cost_estimate=pl.CostEstimate(flops=8 * n * n * columns, bytes_accessed=4 * n * n, transcendentals=0),
        compiler_params=pltpu.CompilerParams(vmem_limit_bytes=32 << 20),
    )(w, split, base)


def split(values):
    high = lax.reduce_precision(values, 8, 7)
    return jnp.concatenate([high.astype(bf16), (values - high).astype(bf16)], axis=1)


def exchanges():
    peers = math.prod(lax.axis_size(axis) for axis in ROWS)
    up = [(i, i + 1) for i in range(1, peers - 1, 2)]
    pairs = up + [(j, i) for i, j in up]

    def outer(array):
        return lax.ppermute(array, ROWS, pairs)

    return outer, swap


def swap(array):
    return lax.ppermute(array, "core", [(0, 1), (1, 0)])


def gathered(part):
    copies = jnp.broadcast_to(part[None], (32,) + part.shape)
    return lax.all_to_all(copies, ("z", "x"), 0, 0)


def moments(parts):
    b00, b01, b02, b03, b11, b12, b13, b22, b23, own = [parts[:, k] for k in range(10)]
    mass = jnp.sum(b00, axis=0)
    shift = jnp.sum(own * b00 + b01, axis=0) / mass
    d = own - shift[None]
    m1 = b01 + d * b00
    m2 = b11 + d * (2 * b01 + d * b00)
    m3 = b12 + d * (2 * b11 + b02 + d * (3 * b01 + d * b00))
    m4 = b22 + d * (4 * b12 + d * (2 * b02 + 4 * b11 + d * (4 * b01 + d * b00)))
    m5 = b23 + d * (
        3 * b22 + 2 * b13 + d * (9 * b12 + b03 + d * (4 * b02 + 6 * b11 + d * (5 * b01 + d * b00)))
    )
    return shift, [mass] + [jnp.sum(m, axis=0) for m in (m1, m2, m3, m4, m5)]


def coefficients(shift, m):
    level = 1.0 - diffusion * shift
    h = [level * m[k] - diffusion * m[k + 1] for k in range(5)]
    least, most = 1.0 / (1.0 + diffusion), 1.0 / (1.0 - diffusion)
    l10 = h[1] / h[0]
    l20 = h[2] / h[0]
    d1 = jnp.maximum(h[2] - l10 * h[1], tiny * h[2])
    e21 = h[3] - l20 * h[1]
    l21 = e21 / d1
    d2 = jnp.maximum(h[4] - l20 * h[2] - l21 * e21, tiny * h[4])
    b0 = m[0]
    b1 = m[1] - l10 * b0
    b2 = m[2] - l20 * b0 - l21 * b1
    y0 = b0 / h[0]
    y1 = diffusion * y0 * jnp.clip(b1 / (d1 * diffusion * y0), least, most)
    y2 = diffusion * y1 * jnp.clip(b2 / (d2 * diffusion * y1), least, most)
    c2 = y2
    c1 = y1 - l21 * c2
    c0 = y0 - l10 * c1 - l20 * c2
    return c0, c1, c2


def powers(shift, g0, g1, g2):
    v1 = g1 - shift * g0
    t1 = g2 - shift * g1
    return v1, t1, t1 - shift * v1


def dots(pairs):
    return jnp.stack([jnp.sum(a * b, axis=0) for a, b in pairs])


def shards(embeddings, neighbours, queries):
    outer, inner = exchanges()
    blocks = neighbours.shape[0]
    index = lax.axis_index(ROWS)
    core = lax.axis_index("core")
    e_out, e_in = outer(embeddings), inner(embeddings)
    q_out, q_in = outer(queries), inner(queries)
    owners = jnp.stack([index, index + 1 - 2 * core, index - 1 + 2 * core])
    candidates = owners[:, None] * blocks + jnp.arange(blocks, dtype=jnp.int32)
    linked = jnp.any(neighbours[None, :, None, :] == candidates[:, None, :, None], axis=3).astype(f32)

    w_own, deg_own = affinity(embeddings, embeddings, linked[0])
    w_in, deg_in = affinity(embeddings, e_in, linked[1])
    w_out, deg_out = affinity(embeddings, e_out, linked[2])
    scale = lax.rsqrt(jnp.sum(deg_own + deg_in + deg_out, axis=1))
    s_out, s_in = outer(scale), inner(scale)
    zero = jnp.zeros_like(queries)
    column = scale[:, None]

    def apply(own, near, far):
        mixed = product(w_own, own, zero)
        mixed = product(w_in, near, mixed)
        return column * product(w_out, far, mixed)

    g0 = queries
    g1 = apply(split(column * g0), split(s_in[:, None] * q_in), split(s_out[:, None] * q_out))
    u1 = split(column * g1)
    u1_out, u1_in = outer(u1), inner(u1)
    early = dots(((g0, g0), (g0, g1)))
    early = early + inner(early)
    own_shift = jnp.clip(jnp.where(early[0] > 0, early[1] / early[0], 0.0), -1.0, 1.0)
    g2 = apply(u1, u1_in, u1_out)
    u2 = split(column * g2)
    u2_out, u2_in = outer(u2), inner(u2)
    g3 = apply(u2, u2_in, u2_out)
    v1, t1, v2 = powers(own_shift, g0, g1, g2)
    v3 = (g3 - own_shift * g2) - own_shift * t1 - own_shift * v2
    part = dots(
        ((g0, g0), (g0, v1), (g0, v2), (g0, v3), (v1, v1), (v1, v2), (v1, v3), (v2, v2), (v2, v3))
    )
    part = part + inner(part)
    shift, m = moments(gathered(jnp.concatenate([part, own_shift[None]])))
    c0, c1, c2 = coefficients(shift, m)
    v1, _, v2 = powers(shift, g0, g1, g2)
    return c0 * g0 + c1 * v1 + c2 * v2


def solution(mesh):
    fine = Mesh(mesh.devices.reshape(8, 4, 2, 4), ("z", "x", "core", "cols"))
    placed = (P(ROWS, None), P(ROWS, None), P(ROWS, "cols"))
    return jax.shard_map(
        shards, mesh=fine, in_specs=placed, out_specs=P(ROWS, "cols"), check_vma=False
    )
```

```python
import math

import jax
import jax.numpy as jnp
from jax import lax
from jax.experimental import pallas as pl
from jax.experimental.pallas import tpu as pltpu
from jax.sharding import Mesh, PartitionSpec as P


diffusion = 0.9
epsilon = 1e-06
tiny = 2e-07
smallest = 1e-37
f32 = jnp.float32
bf16 = jnp.bfloat16
ROWS = ("z", "x", "core")


def unit_rows(raw):
    values = raw.astype(f32)
    total = jnp.sum(values * values, axis=1, keepdims=True)
    return (values * lax.rsqrt(total + epsilon)).astype(bf16)


VECTOR = pl.BlockSpec(memory_space=pltpu.VMEM)
SCALAR = pl.BlockSpec(memory_space=pltpu.SMEM)


def kernel_call(kernel, scalars, arrays, outs, flops, moved, scratch=()):
    return pl.pallas_call(
        kernel,
        in_specs=[SCALAR] * len(scalars) + [VECTOR] * len(arrays),
        out_specs=[VECTOR] * len(outs),
        out_shape=[jax.ShapeDtypeStruct(*out) for out in outs],
        scratch_shapes=scratch,
        cost_estimate=pl.CostEstimate(flops=flops, bytes_accessed=moved, transcendentals=0),
        compiler_params=pltpu.CompilerParams(vmem_limit_bytes=16 << 20),
    )(*scalars, *arrays)


def affinity_kernel(neighbours, first, unit_ref, other_ref, w_ref, sums_ref, across_ref=None):
    blocks, slots = neighbours.shape
    rows = unit_ref.shape[0] // blocks
    half = rows // 2
    sums_ref[...] = jnp.zeros_like(sums_ref)
    for c in range(blocks):
        columns = pl.ds(c * rows, rows)
        other = other_ref[columns, :] if other_ref is unit_ref else unit_rows(other_ref[columns, :])
        across = None
        for b in range(blocks):
            linked = neighbours[b, 0] == first[0] + c
            for k in range(1, slots):
                linked = linked | (neighbours[b, k] == first[0] + c)
            similar = lax.dot_general(
                unit_ref[pl.ds(b * rows, rows), :],
                other,
                (((1,), (1,)), ((), ())),
                preferred_element_type=f32,
            )
            kept = jnp.maximum(similar, 0.0)
            w = kept * kept * (kept * jnp.where(linked, 1.0, 0.0).astype(f32))
            high = w.astype(bf16)
            w_ref[pl.ds(2 * b * rows, rows), columns] = high
            w_ref[pl.ds((2 * b + 1) * rows, rows), columns] = (w - high.astype(f32)).astype(bf16)
            sums_ref[pl.ds(b * rows, rows), :] += w[:, :half] + w[:, half:]
            if across_ref is not None:
                folded = jnp.sum(w.reshape(rows // 8, 8, rows), axis=0)
                across = folded if across is None else across + folded
        if across_ref is not None:
            across_ref[:, columns] = across


def own_affinity_kernel(neighbours, first, raw_ref, w_ref, sums_ref, unit_ref):
    unit_ref[...] = unit_rows(raw_ref[...])
    affinity_kernel(neighbours, first, unit_ref, unit_ref, w_ref, sums_ref)


def affinity(neighbours, block, own, other=None, both=False):
    n, features = own.shape
    outs = [((2 * n, n), bf16), ((n, 128), f32)]
    if other is None:
        outs.append(((n, features), bf16))
    if both:
        outs.append(((8, n), f32))
    return kernel_call(
        own_affinity_kernel if other is None else affinity_kernel,
        (neighbours, block.reshape(1)),
        (own,) if other is None else (own, other),
        outs,
        2 * n * n * features,
        8 * n * n,
    )


def product_kernel(w_ref, u_ref, base_ref, out_ref):
    n, columns = out_ref.shape
    rows = n // 4
    for b in range(4):
        part = pl.ds(b * rows, rows)
        wide = jnp.dot(w_ref[pl.ds(2 * b * rows, 2 * rows), :], u_ref[...], preferred_element_type=f32)
        both = wide[:rows] + wide[rows:]
        if u_ref.shape[1] > columns:
            both = both[:, :columns] + both[:, columns:]
        out_ref[part, :] = base_ref[part, :] + both


def first_product_kernel(w_ref, v_ref, scale_ref, base_ref, out_ref, u_ref):
    columns = v_ref.shape[1]
    values = v_ref[...] * scale_ref[...]
    high = values.astype(bf16)
    u_ref[:, :columns] = high
    u_ref[:, columns:] = (values - high.astype(f32)).astype(bf16)
    product_kernel(w_ref, u_ref, base_ref, out_ref)


def first_product(w, v, scale, base):
    n, columns = base.shape
    (out,) = kernel_call(
        first_product_kernel,
        (),
        (w, v, scale, base),
        [((n, columns), f32)],
        8 * n * n * columns,
        4 * n * n,
        scratch=[pltpu.VMEM((n, 2 * columns), bf16)],
    )
    return out


def product(w, split, base):
    n, columns = base.shape
    (out,) = kernel_call(
        product_kernel, (), (w, split, base), [((n, columns), f32)], 8 * n * n * columns, 4 * n * n
    )
    return out


def split(values):
    high = lax.reduce_precision(values, 8, 7)
    return jnp.concatenate([high.astype(bf16), (values - high).astype(bf16)], axis=1)


def outward(array):
    peers = math.prod(lax.axis_size(axis) for axis in ROWS)
    up = [(i, i + 1) for i in range(1, peers - 1, 2)]
    return lax.ppermute(array, ROWS, up + [(j, i) for i, j in up])


def swap(array):
    return lax.ppermute(array, "core", [(0, 1), (1, 0)])


def gathered(part):
    copies = jnp.broadcast_to(part[None], (32,) + part.shape).reshape(32, -1, 2, part.shape[1])
    return lax.all_to_all(copies, ("z", "x"), 0, 0).reshape((32,) + part.shape)


PAIRS = ((0, 0), (0, 1), (0, 2), (0, 3), (1, 1), (1, 2), (1, 3), (2, 2), (2, 3))
CHAIN = ((0, 0), (0, 1), (1, 1), (1, 2), (2, 2), (2, 3))


def moved(sums, d, pairs):
    powers = [jnp.ones_like(d)]
    for _ in range(5):
        powers.append(powers[-1] * d)
    out = {}
    for i, j in pairs:
        terms = [
            math.comb(i, a) * math.comb(j, c) * powers[i - a + j - c] * sums[min(a, c), max(a, c)]
            for a in range(i, -1, -1)
            for c in range(j, -1, -1)
        ]
        out[i, j] = sum(terms[1:], terms[0])
    return out


def unpacked(part):
    rows = [part[..., k, :] for k in range(len(PAIRS) + 1)]
    return dict(zip(PAIRS, rows)), rows[-1]


def both_cores(part):
    mine, my_shift = unpacked(part)
    theirs, their_shift = unpacked(swap(part))
    shift = 0.5 * (my_shift + their_shift)
    mine = moved(mine, my_shift - shift, PAIRS)
    theirs = moved(theirs, their_shift - shift, PAIRS)
    return jnp.stack([mine[p] + theirs[p] for p in PAIRS] + [shift])


def moments(parts):
    sums, own = unpacked(parts)
    mass = jnp.sum(sums[0, 0], axis=0)
    shift = jnp.sum(own * sums[0, 0] + sums[0, 1], axis=0) / mass
    central = moved(sums, own - shift[None], CHAIN)
    return shift, [jnp.sum(central[p], axis=0) for p in CHAIN]


def coefficients(shift, m):
    level = 1.0 - diffusion * shift
    h = [level * m[k] - diffusion * m[k + 1] for k in range(5)]
    least, most = 1.0 / (1.0 + diffusion), 1.0 / (1.0 - diffusion)
    l10 = h[1] / h[0]
    l20 = h[2] / h[0]
    d1 = jnp.maximum(h[2] - l10 * h[1], tiny * h[2])
    e21 = h[3] - l20 * h[1]
    l21 = e21 / d1
    d2 = jnp.maximum(h[4] - l20 * h[2] - l21 * e21, tiny * h[4])
    b0 = m[0]
    b1 = m[1] - l10 * b0
    b2 = m[2] - l20 * b0 - l21 * b1
    y0 = b0 / h[0]
    y1 = diffusion * y0 * jnp.clip(b1 / (d1 * diffusion * y0), least, most)
    y2 = diffusion * y1 * jnp.clip(b2 / (d2 * diffusion * y1), least, most)
    c2 = y2
    c1 = y1 - l21 * c2
    c0 = y0 - l10 * c1 - l20 * c2
    return c0, c1, c2


def powers(shift, g0, g1, g2):
    v1 = g1 - shift * g0
    t1 = g2 - shift * g1
    return v1, t1, t1 - shift * v1


def diffuse(embeddings, neighbours, queries):
    e_out, e_in = outward(embeddings), swap(embeddings)
    q_out, q_in = outward(queries), swap(queries)
    columns = queries.shape[1]
    blocks = neighbours.shape[0]
    index = lax.axis_index(ROWS)
    core = lax.axis_index("core")
    near, far = (index + 1 - 2 * core) * blocks, (index - 1 + 2 * core) * blocks
    w_own, deg_own, unit = affinity(neighbours, index * blocks, embeddings)
    w_in, deg_in = affinity(neighbours, near, unit, e_in)
    chip = jnp.sum(deg_own + deg_in, axis=1)
    unit, chip = lax.optimization_barrier((unit, chip))
    chip_out = outward(chip)
    w_out, deg_out, across = affinity(neighbours, far, unit, e_out, both=True)
    degree = chip + jnp.sum(jnp.maximum(deg_out, 0.0), axis=1)
    degree_in = swap(degree)
    degree_out = chip_out + jnp.sum(jnp.maximum(across, 0.0), axis=0)

    def wide_scale(sums):
        return lax.rsqrt(jnp.broadcast_to(jnp.maximum(sums, smallest)[:, None], queries.shape))

    column = wide_scale(degree)
    zero = jnp.zeros_like(queries)

    def apply(own, outer, inner):
        mixed = product(w_own, own, zero)
        mixed = product(w_in, inner, mixed)
        return column * product(w_out, outer, mixed)

    g0 = queries
    mixed = first_product(w_own, g0, column, zero)
    mixed = first_product(w_in, q_in, wide_scale(degree_in), mixed)
    g1 = column * first_product(w_out, q_out, wide_scale(degree_out), mixed)
    u1 = split(column * g1)
    g2 = apply(u1, outward(u1), swap(u1))
    u2 = split(column * g2)
    g3 = apply(u2, outward(u2[:, :columns]), swap(u2))
    mass, slope = jnp.sum(g0 * g0, axis=0), jnp.sum(g0 * g1, axis=0)
    own_shift = jnp.clip(jnp.where(mass > 0, slope / mass, 0.0), -1.0, 1.0)
    v1, t1, v2 = powers(own_shift, g0, g1, g2)
    v3 = (g3 - own_shift * g2) - own_shift * t1 - own_shift * v2
    v = (g0, v1, v2, v3)
    part = jnp.stack([jnp.sum(v[i] * v[j], axis=0) for i, j in PAIRS] + [own_shift])
    shift, m = moments(gathered(both_cores(part)))
    c0, c1, c2 = coefficients(shift, m)
    v1, _, v2 = powers(shift, g0, g1, g2)
    return c0 * g0 + c1 * v1 + c2 * v2


def solution(mesh):
    fine = Mesh(mesh.devices.reshape(8, 4, 2, 4), ("z", "x", "core", "cols"))
    placed = (P(ROWS, None), P(ROWS, None), P(ROWS, "cols"))
    return jax.shard_map(
        diffuse, mesh=fine, in_specs=placed, out_specs=P(ROWS, "cols"), check_vma=False
    )
```

```python
import math

import jax
import jax.numpy as jnp
from jax import lax
from jax.experimental import pallas as pl
from jax.experimental.pallas import tpu as pltpu
from jax.sharding import Mesh, PartitionSpec as P


diffusion = 0.9
epsilon = 1e-06
tiny = 2e-07
smallest = 1e-37
f32 = jnp.float32
bf16 = jnp.bfloat16
ROWS = ("z", "x", "core")


def unit_rows(raw):
    values = raw.astype(f32)
    total = jnp.sum(values * values, axis=1, keepdims=True)
    return (values * lax.rsqrt(total + epsilon)).astype(bf16)


VECTOR = pl.BlockSpec(memory_space=pltpu.VMEM)
SCALAR = pl.BlockSpec(memory_space=pltpu.SMEM)


def kernel_call(kernel, scalars, arrays, outs, flops, moved, scratch=()):
    return pl.pallas_call(
        kernel,
        in_specs=[SCALAR] * len(scalars) + [VECTOR] * len(arrays),
        out_specs=[VECTOR] * len(outs),
        out_shape=[jax.ShapeDtypeStruct(*out) for out in outs],
        scratch_shapes=scratch,
        cost_estimate=pl.CostEstimate(flops=flops, bytes_accessed=moved, transcendentals=0),
        compiler_params=pltpu.CompilerParams(vmem_limit_bytes=16 << 20),
    )(*scalars, *arrays)


def affinity_kernel(neighbours, first, unit_ref, other_ref, w_ref, sums_ref, across_ref=None):
    blocks, slots = neighbours.shape
    rows = unit_ref.shape[0] // blocks
    half = rows // 2
    sums_ref[...] = jnp.zeros_like(sums_ref)
    for c in range(blocks):
        columns = pl.ds(c * rows, rows)
        other = other_ref[columns, :] if other_ref is unit_ref else unit_rows(other_ref[columns, :])
        across = None
        for b in range(blocks):
            linked = neighbours[b, 0] == first[0] + c
            for k in range(1, slots):
                linked = linked | (neighbours[b, k] == first[0] + c)
            similar = lax.dot_general(
                unit_ref[pl.ds(b * rows, rows), :],
                other,
                (((1,), (1,)), ((), ())),
                preferred_element_type=f32,
            )
            kept = jnp.maximum(similar, 0.0)
            w = kept * kept * (kept * jnp.where(linked, 1.0, 0.0).astype(f32))
            high = w.astype(bf16)
            w_ref[pl.ds(2 * b * rows, rows), columns] = high
            w_ref[pl.ds((2 * b + 1) * rows, rows), columns] = (w - high.astype(f32)).astype(bf16)
            sums_ref[pl.ds(b * rows, rows), :] += w[:, :half] + w[:, half:]
            if across_ref is not None:
                folded = jnp.sum(w.reshape(rows // 8, 8, rows), axis=0)
                across = folded if across is None else across + folded
        if across_ref is not None:
            across_ref[:, columns] = across


def own_affinity_kernel(neighbours, first, raw_ref, w_ref, sums_ref, unit_ref):
    unit_ref[...] = unit_rows(raw_ref[...])
    affinity_kernel(neighbours, first, unit_ref, unit_ref, w_ref, sums_ref)


def affinity(neighbours, block, own, other=None, both=False):
    n, features = own.shape
    outs = [((2 * n, n), bf16), ((n, 128), f32)]
    if other is None:
        outs.append(((n, features), bf16))
    if both:
        outs.append(((8, n), f32))
    return kernel_call(
        own_affinity_kernel if other is None else affinity_kernel,
        (neighbours, block.reshape(1)),
        (own,) if other is None else (own, other),
        outs,
        2 * n * n * features,
        8 * n * n,
    )


def product_kernel(w_ref, u_ref, base_ref, out_ref):
    n, columns = out_ref.shape
    rows = n // 4
    for b in range(4):
        part = pl.ds(b * rows, rows)
        if u_ref.shape[1] > columns:
            stacked = w_ref[pl.ds(2 * b * rows, 2 * rows), :]
            wide = jnp.dot(stacked, u_ref[...], preferred_element_type=f32)
            both = wide[:rows] + wide[rows:]
            both = both[:, :columns] + both[:, columns:]
        else:
            high = w_ref[pl.ds(2 * b * rows, rows), :]
            both = jnp.dot(high, u_ref[...], preferred_element_type=f32)
        out_ref[part, :] = base_ref[part, :] + both


def first_product_kernel(w_ref, v_ref, scale_ref, base_ref, out_ref, u_ref):
    columns = v_ref.shape[1]
    values = v_ref[...] * scale_ref[...]
    high = values.astype(bf16)
    u_ref[:, :columns] = high
    u_ref[:, columns:] = (values - high.astype(f32)).astype(bf16)
    product_kernel(w_ref, u_ref, base_ref, out_ref)


def first_product(w, v, scale, base):
    n, columns = base.shape
    (out,) = kernel_call(
        first_product_kernel,
        (),
        (w, v, scale, base),
        [((n, columns), f32)],
        8 * n * n * columns,
        4 * n * n,
        scratch=[pltpu.VMEM((n, 2 * columns), bf16)],
    )
    return out


def product(w, split, base):
    n, columns = base.shape
    (out,) = kernel_call(
        product_kernel, (), (w, split, base), [((n, columns), f32)], 8 * n * n * columns, 4 * n * n
    )
    return out


def split(values):
    high = lax.reduce_precision(values, 8, 7)
    return jnp.concatenate([high.astype(bf16), (values - high).astype(bf16)], axis=1)


def outward(array):
    peers = math.prod(lax.axis_size(axis) for axis in ROWS)
    up = [(i, i + 1) for i in range(1, peers - 1, 2)]
    return lax.ppermute(array, ROWS, up + [(j, i) for i, j in up])


def swap(array):
    return lax.ppermute(array, "core", [(0, 1), (1, 0)])


def gathered(part):
    copies = jnp.broadcast_to(part[None], (32,) + part.shape).reshape(32, -1, 2, part.shape[1])
    return lax.all_to_all(copies, ("z", "x"), 0, 0).reshape((32,) + part.shape)


PAIRS = ((0, 0), (0, 1), (0, 2), (0, 3), (1, 1), (1, 2), (1, 3), (2, 2), (2, 3))
CHAIN = ((0, 0), (0, 1), (1, 1), (1, 2), (2, 2), (2, 3))


def moved(sums, d, pairs):
    powers = [jnp.ones_like(d)]
    for _ in range(5):
        powers.append(powers[-1] * d)
    out = {}
    for i, j in pairs:
        terms = [
            math.comb(i, a) * math.comb(j, c) * powers[i - a + j - c] * sums[min(a, c), max(a, c)]
            for a in range(i, -1, -1)
            for c in range(j, -1, -1)
        ]
        out[i, j] = sum(terms[1:], terms[0])
    return out


def unpacked(part):
    rows = [part[..., k, :] for k in range(len(PAIRS) + 1)]
    return dict(zip(PAIRS, rows)), rows[-1]


def both_cores(part):
    mine, my_shift = unpacked(part)
    theirs, their_shift = unpacked(swap(part))
    shift = 0.5 * (my_shift + their_shift)
    mine = moved(mine, my_shift - shift, PAIRS)
    theirs = moved(theirs, their_shift - shift, PAIRS)
    return jnp.stack([mine[p] + theirs[p] for p in PAIRS] + [shift])


def moments(parts):
    sums, own = unpacked(parts)
    mass = jnp.sum(sums[0, 0], axis=0)
    shift = jnp.sum(own * sums[0, 0] + sums[0, 1], axis=0) / mass
    central = moved(sums, own - shift[None], CHAIN)
    return shift, [jnp.sum(central[p], axis=0) for p in CHAIN]


def coefficients(shift, m):
    level = 1.0 - diffusion * shift
    h = [level * m[k] - diffusion * m[k + 1] for k in range(5)]
    least, most = 1.0 / (1.0 + diffusion), 1.0 / (1.0 - diffusion)
    l10 = h[1] / h[0]
    l20 = h[2] / h[0]
    d1 = jnp.maximum(h[2] - l10 * h[1], tiny * h[2])
    e21 = h[3] - l20 * h[1]
    l21 = e21 / d1
    d2 = jnp.maximum(h[4] - l20 * h[2] - l21 * e21, tiny * h[4])
    b0 = m[0]
    b1 = m[1] - l10 * b0
    b2 = m[2] - l20 * b0 - l21 * b1
    y0 = b0 / h[0]
    y1 = diffusion * y0 * jnp.clip(b1 / (d1 * diffusion * y0), least, most)
    y2 = diffusion * y1 * jnp.clip(b2 / (d2 * diffusion * y1), least, most)
    c2 = y2
    c1 = y1 - l21 * c2
    c0 = y0 - l10 * c1 - l20 * c2
    return c0, c1, c2


def powers(shift, g0, g1, g2):
    v1 = g1 - shift * g0
    t1 = g2 - shift * g1
    return v1, t1, t1 - shift * v1


def diffuse(embeddings, neighbours, queries):
    e_out, e_in = outward(embeddings), swap(embeddings)
    q_out, q_in = outward(queries), swap(queries)
    columns = queries.shape[1]
    blocks = neighbours.shape[0]
    index = lax.axis_index(ROWS)
    core = lax.axis_index("core")
    near, far = (index + 1 - 2 * core) * blocks, (index - 1 + 2 * core) * blocks
    w_own, deg_own, unit = affinity(neighbours, index * blocks, embeddings)
    w_in, deg_in = affinity(neighbours, near, unit, e_in)
    chip = jnp.sum(deg_own + deg_in, axis=1)
    unit, chip = lax.optimization_barrier((unit, chip))
    chip_out = outward(chip)
    w_out, deg_out, across = affinity(neighbours, far, unit, e_out, both=True)
    degree = chip + jnp.sum(jnp.maximum(deg_out, 0.0), axis=1)
    degree_in = swap(degree)
    degree_out = chip_out + jnp.sum(jnp.maximum(across, 0.0), axis=0)

    def wide_scale(sums):
        return lax.rsqrt(jnp.broadcast_to(jnp.maximum(sums, smallest)[:, None], queries.shape))

    column = wide_scale(degree)
    zero = jnp.zeros_like(queries)

    def apply(own, outer, inner):
        mixed = product(w_own, own, zero)
        mixed = product(w_in, inner, mixed)
        return column * product(w_out, outer, mixed)

    g0 = queries
    mixed = first_product(w_own, g0, column, zero)
    mixed = first_product(w_in, q_in, wide_scale(degree_in), mixed)
    g1 = column * first_product(w_out, q_out, wide_scale(degree_out), mixed)
    u1 = split(column * g1)
    g2 = apply(u1, outward(u1), swap(u1))
    u2 = split(column * g2)
    u2_out, u2_in = outward(u2[:, :columns]), swap(u2)
    g1, g2, u2 = lax.optimization_barrier((g1, g2, u2))
    mass, slope = jnp.sum(g0 * g0, axis=0), jnp.sum(g0 * g1, axis=0)
    own_shift = jnp.clip(jnp.where(mass > 0, slope / mass, 0.0), -1.0, 1.0)
    v1, t1, v2 = powers(own_shift, g0, g1, g2)
    v = (g0, v1, v2, own_shift * (g2 + t1 + v2))
    sums = {(i, j): jnp.sum(v[i] * v[j], axis=0) for i, j in PAIRS if j < 3}
    v, sums = lax.optimization_barrier((v, sums))
    g3 = apply(u2, u2_out, u2_in)
    v3 = g3 - v[3]
    sums.update({(i, 3): jnp.sum(v[i] * v3, axis=0) for i in range(3)})
    part = jnp.stack([sums[p] for p in PAIRS] + [own_shift])
    shift, m = moments(gathered(both_cores(part)))
    c0, c1, c2 = coefficients(shift, m)
    v1, _, v2 = powers(shift, g0, g1, g2)
    return c0 * g0 + c1 * v1 + c2 * v2


def solution(mesh):
    fine = Mesh(mesh.devices.reshape(8, 4, 2, 4), ("z", "x", "core", "cols"))
    placed = (P(ROWS, None), P(ROWS, None), P(ROWS, "cols"))
    return jax.shard_map(
        diffuse, mesh=fine, in_specs=placed, out_specs=P(ROWS, "cols"), check_vma=False
    )
```

```python
import math

import jax
import jax.numpy as jnp
from jax import lax
from jax.experimental import pallas as pl
from jax.experimental.pallas import tpu as pltpu
from jax.sharding import Mesh, PartitionSpec as P


diffusion = 0.9
epsilon = 1e-06
tiny = 2e-07
smallest = 1e-37
f32 = jnp.float32
bf16 = jnp.bfloat16
ROWS = ("z", "x", "core")


def unit_rows(raw):
    values = raw.astype(f32)
    total = jnp.sum(values * values, axis=1, keepdims=True)
    return (values * lax.rsqrt(total + epsilon)).astype(bf16)


VECTOR = pl.BlockSpec(memory_space=pltpu.VMEM)
SCALAR = pl.BlockSpec(memory_space=pltpu.SMEM)


def kernel_call(kernel, scalars, arrays, outs, flops, moved, scratch=()):
    return pl.pallas_call(
        kernel,
        in_specs=[SCALAR] * len(scalars) + [VECTOR] * len(arrays),
        out_specs=[VECTOR] * len(outs),
        out_shape=[jax.ShapeDtypeStruct(*out) for out in outs],
        scratch_shapes=scratch,
        cost_estimate=pl.CostEstimate(flops=flops, bytes_accessed=moved, transcendentals=0),
        compiler_params=pltpu.CompilerParams(vmem_limit_bytes=16 << 20),
    )(*scalars, *arrays)


def affinity_kernel(neighbours, first, unit_ref, other_ref, w_ref, sums_ref, across_ref=None):
    blocks, slots = neighbours.shape
    rows = unit_ref.shape[0] // blocks
    half = rows // 2
    sums_ref[...] = jnp.zeros_like(sums_ref)
    for c in range(blocks):
        columns = pl.ds(c * rows, rows)
        other = other_ref[columns, :] if other_ref is unit_ref else unit_rows(other_ref[columns, :])
        across = None
        for b in range(blocks):
            linked = neighbours[b, 0] == first[0] + c
            for k in range(1, slots):
                linked = linked | (neighbours[b, k] == first[0] + c)
            similar = lax.dot_general(
                unit_ref[pl.ds(b * rows, rows), :],
                other,
                (((1,), (1,)), ((), ())),
                preferred_element_type=f32,
            )
            kept = jnp.maximum(similar, 0.0)
            w = kept * kept * (kept * jnp.where(linked, 1.0, 0.0).astype(f32))
            high = w.astype(bf16)
            w_ref[pl.ds(2 * b * rows, rows), columns] = high
            w_ref[pl.ds((2 * b + 1) * rows, rows), columns] = (w - high.astype(f32)).astype(bf16)
            sums_ref[pl.ds(b * rows, rows), :] += w[:, :half] + w[:, half:]
            if across_ref is not None:
                folded = jnp.sum(w.reshape(rows // 8, 8, rows), axis=0)
                across = folded if across is None else across + folded
        if across_ref is not None:
            across_ref[:, columns] = across


def own_affinity_kernel(neighbours, first, raw_ref, w_ref, sums_ref, unit_ref):
    unit_ref[...] = unit_rows(raw_ref[...])
    affinity_kernel(neighbours, first, unit_ref, unit_ref, w_ref, sums_ref)


def affinity(neighbours, block, own, other=None, both=False):
    n, features = own.shape
    outs = [((2 * n, n), bf16), ((n, 128), f32)]
    if other is None:
        outs.append(((n, features), bf16))
    if both:
        outs.append(((8, n), f32))
    return kernel_call(
        own_affinity_kernel if other is None else affinity_kernel,
        (neighbours, block.reshape(1)),
        (own,) if other is None else (own, other),
        outs,
        2 * n * n * features,
        8 * n * n,
    )


def product_kernel(w_ref, u_ref, base_ref, out_ref):
    n, columns = out_ref.shape
    rows = n // 4
    for b in range(4):
        part = pl.ds(b * rows, rows)
        if u_ref.shape[1] > columns:
            stacked = w_ref[pl.ds(2 * b * rows, 2 * rows), :]
            wide = jnp.dot(stacked, u_ref[...], preferred_element_type=f32)
            both = wide[:rows] + wide[rows:]
            both = both[:, :columns] + both[:, columns:]
        else:
            high = w_ref[pl.ds(2 * b * rows, rows), :]
            both = jnp.dot(high, u_ref[...], preferred_element_type=f32)
        out_ref[part, :] = both if base_ref is None else base_ref[part, :] + both


def bare_product_kernel(w_ref, u_ref, out_ref):
    product_kernel(w_ref, u_ref, None, out_ref)


def first_product_kernel(w_ref, v_ref, scale_ref, base_ref, out_ref, u_ref):
    columns = v_ref.shape[1]
    values = v_ref[...] * scale_ref[...]
    high = values.astype(bf16)
    u_ref[:, :columns] = high
    u_ref[:, columns:] = (values - high.astype(f32)).astype(bf16)
    product_kernel(w_ref, u_ref, base_ref, out_ref)


def bare_first_product_kernel(w_ref, v_ref, scale_ref, out_ref, u_ref):
    first_product_kernel(w_ref, v_ref, scale_ref, None, out_ref, u_ref)


def first_product(w, v, scale, *base):
    n, columns = v.shape
    (out,) = kernel_call(
        first_product_kernel if base else bare_first_product_kernel,
        (),
        (w, v, scale) + base,
        [((n, columns), f32)],
        8 * n * n * columns,
        4 * n * n,
        scratch=[pltpu.VMEM((n, 2 * columns), bf16)],
    )
    return out


def product(w, split, columns, *base):
    n = w.shape[1]
    (out,) = kernel_call(
        product_kernel if base else bare_product_kernel,
        (),
        (w, split) + base,
        [((n, columns), f32)],
        8 * n * n * columns,
        4 * n * n,
    )
    return out


def split(values):
    high = lax.reduce_precision(values, 8, 7)
    return jnp.concatenate([high.astype(bf16), (values - high).astype(bf16)], axis=1)


def outward(array):
    peers = math.prod(lax.axis_size(axis) for axis in ROWS)
    up = [(i, i + 1) for i in range(1, peers - 1, 2)]
    return lax.ppermute(array, ROWS, up + [(j, i) for i, j in up])


def swap(array):
    return lax.ppermute(array, "core", [(0, 1), (1, 0)])


def gathered(part):
    copies = jnp.broadcast_to(part[None], (32,) + part.shape).reshape(32, -1, 2, part.shape[1])
    return lax.all_to_all(copies, ("z", "x"), 0, 0).reshape((32,) + part.shape)


PAIRS = ((0, 0), (0, 1), (0, 2), (0, 3), (1, 1), (1, 2), (1, 3), (2, 2), (2, 3))
CHAIN = ((0, 0), (0, 1), (1, 1), (1, 2), (2, 2), (2, 3))


def moved(sums, d, pairs):
    powers = [jnp.ones_like(d)]
    for _ in range(5):
        powers.append(powers[-1] * d)
    out = {}
    for i, j in pairs:
        terms = [
            math.comb(i, a) * math.comb(j, c) * powers[i - a + j - c] * sums[min(a, c), max(a, c)]
            for a in range(i, -1, -1)
            for c in range(j, -1, -1)
        ]
        out[i, j] = sum(terms[1:], terms[0])
    return out


def unpacked(part):
    rows = [part[..., k, :] for k in range(len(PAIRS) + 1)]
    return dict(zip(PAIRS, rows)), rows[-1]


def both_cores(part):
    mine, my_shift = unpacked(part)
    theirs, their_shift = unpacked(swap(part))
    shift = 0.5 * (my_shift + their_shift)
    mine = moved(mine, my_shift - shift, PAIRS)
    theirs = moved(theirs, their_shift - shift, PAIRS)
    return jnp.stack([mine[p] + theirs[p] for p in PAIRS] + [shift])


def moments(parts):
    sums, own = unpacked(parts)
    mass = jnp.sum(sums[0, 0], axis=0)
    shift = jnp.sum(own * sums[0, 0] + sums[0, 1], axis=0) / mass
    central = moved(sums, own - shift[None], CHAIN)
    return shift, [jnp.sum(central[p], axis=0) for p in CHAIN]


def coefficients(shift, m):
    level = 1.0 - diffusion * shift
    h = [level * m[k] - diffusion * m[k + 1] for k in range(5)]
    least, most = 1.0 / (1.0 + diffusion), 1.0 / (1.0 - diffusion)
    l10 = h[1] / h[0]
    l20 = h[2] / h[0]
    d1 = jnp.maximum(h[2] - l10 * h[1], tiny * h[2])
    e21 = h[3] - l20 * h[1]
    l21 = e21 / d1
    d2 = jnp.maximum(h[4] - l20 * h[2] - l21 * e21, tiny * h[4])
    b0 = m[0]
    b1 = m[1] - l10 * b0
    b2 = m[2] - l20 * b0 - l21 * b1
    y0 = b0 / h[0]
    y1 = diffusion * y0 * jnp.clip(b1 / (d1 * diffusion * y0), least, most)
    y2 = diffusion * y1 * jnp.clip(b2 / (d2 * diffusion * y1), least, most)
    c2 = y2
    c1 = y1 - l21 * c2
    c0 = y0 - l10 * c1 - l20 * c2
    return c0, c1, c2


def powers(shift, g0, g1, g2):
    v1 = g1 - shift * g0
    t1 = g2 - shift * g1
    return v1, t1, t1 - shift * v1


def diffuse(embeddings, neighbours, queries):
    e_out, e_in = outward(embeddings), swap(embeddings)
    q_out, q_in = outward(queries), swap(queries)
    columns = queries.shape[1]
    blocks = neighbours.shape[0]
    index = lax.axis_index(ROWS)
    core = lax.axis_index("core")
    near, far = (index + 1 - 2 * core) * blocks, (index - 1 + 2 * core) * blocks
    w_own, deg_own, unit = affinity(neighbours, index * blocks, embeddings)
    w_in, deg_in = affinity(neighbours, near, unit, e_in)
    chip = jnp.sum(deg_own + deg_in, axis=1)
    unit, chip = lax.optimization_barrier((unit, chip))
    chip_out = outward(chip)
    w_out, deg_out, across = affinity(neighbours, far, unit, e_out, both=True)
    degree = chip + jnp.sum(jnp.maximum(deg_out, 0.0), axis=1)
    degree_in = swap(degree)
    degree_out = chip_out + jnp.sum(jnp.maximum(across, 0.0), axis=0)

    def wide_scale(sums):
        return lax.rsqrt(jnp.broadcast_to(jnp.maximum(sums, smallest)[:, None], queries.shape))

    column = wide_scale(degree)

    def apply(own, outer, inner):
        mixed = product(w_own, own, columns)
        mixed = product(w_in, inner, columns, mixed)
        return column * product(w_out, outer, columns, mixed)

    g0 = queries
    mixed = first_product(w_own, g0, column)
    mixed = first_product(w_in, q_in, wide_scale(degree_in), mixed)
    g1 = column * first_product(w_out, q_out, wide_scale(degree_out), mixed)
    u1 = split(column * g1)
    g2 = apply(u1, outward(u1), swap(u1))
    u2 = split(column * g2)
    u2_out, u2_in = outward(u2[:, :columns]), swap(u2)
    g1, g2, u2 = lax.optimization_barrier((g1, g2, u2))
    mass, slope = jnp.sum(g0 * g0, axis=0), jnp.sum(g0 * g1, axis=0)
    own_shift = jnp.clip(jnp.where(mass > 0, slope / mass, 0.0), -1.0, 1.0)
    v1, t1, v2 = powers(own_shift, g0, g1, g2)
    v = (g0, v1, v2, own_shift * (g2 + t1 + v2))
    sums = {(i, j): jnp.sum(v[i] * v[j], axis=0) for i, j in PAIRS if j < 3}
    v, sums = lax.optimization_barrier((v, sums))
    g3 = apply(u2, u2_out, u2_in)
    v3 = g3 - v[3]
    sums.update({(i, 3): jnp.sum(v[i] * v3, axis=0) for i in range(3)})
    part = jnp.stack([sums[p] for p in PAIRS] + [own_shift])
    shift, m = moments(gathered(both_cores(part)))
    c0, c1, c2 = coefficients(shift, m)
    v1, _, v2 = powers(shift, g0, g1, g2)
    return c0 * g0 + c1 * v1 + c2 * v2


def solution(mesh):
    fine = Mesh(mesh.devices.reshape(8, 4, 2, 4), ("z", "x", "core", "cols"))
    placed = (P(ROWS, None), P(ROWS, None), P(ROWS, "cols"))
    return jax.shard_map(
        diffuse, mesh=fine, in_specs=placed, out_specs=P(ROWS, "cols"), check_vma=False
    )
```
